512 devices in a mesh: tm: 32 (over y, z_hi, core), space: 16 (over x, z_lo).
Axes of the slice: x: 4, y: 8, z: 8 (z_hi: 2, z_lo: 4; z = z_hi * 4 + z_lo), core: 2. Of those that a mesh axis runs over, the one named last changes fastest.
Arguments:
- opening_guess_profile: float32 [32, 64, 128, 256], P('tm', 'space'), may hold values from -6 to 6
- capacity: float32 [64, 128, 256], P('space'), may hold values from 0.25 to 4
- thermal_forcing: float32 [32, 64, 128, 256], P('tm', 'space'), may hold values from -3 to 3
- rough_decay_factor: float32 [32, 64, 128, 256], P('tm', 'space'), may hold values from 0.2 to 1
- tile_ids: int32 [256, 128], P('tm', 'space'), may hold values from 0 to 2047, as said below
- tile_count: int32 [256, 16], P('tm', 'space'), may hold values from 2 to 8, as said below
- tile_blocks: float32 [256, 128, 64, 64], P('tm', 'space'), may hold values from -0.25 to 0.25
Outputs:
- updated_opening_state: float32 [32, 64, 128, 256], P('tm', 'space')
- accurate_ending_thermal_state: float32 [32, 64, 128, 256], P('tm', 'space')
The draws below stay inside these ranges and needn't reach their ends.
Inputs may be any that keep to these rules, and one draw needn't show every extreme that they name: `tile_ids`: the 8 entries of one brick for one step are distinct tile numbers of that brick. `tile_count`: on every brick of every slab some step uses all 8 slots.
All inputs are finite; a program needn't handle non-finite values.
Results may differ from the reference program's by a relative error of at most 0.0003.
Values sent between devices are 32-bit elements; how exact they have to be, the bound alone decides.
A program may use at most 128 MiB of HBM per device.

```python
import math
import jax
import jax.numpy as jnp
from jax import lax

NY = 128
NZ = 256
INCREMENTS = 8
SWEEPS = 4
TILE = 64
MAXT = 8
NX = 64
TILES_DEV = 2048
N_TM = 32
N_SPACE = 16


def draw_rough_decay_factor(key, part):
    key_one, random_key_second, random_key_third = jax.random.split(key, 3)
    shape = (N_TM, NX, NY, NZ)
    exponent = jax.random.uniform(key_one, shape, jnp.float32, -3.0, -0.3)
    rough_estimate = 1.0 - jnp.power(10.0, exponent)
    slab_groups_total = jax.random.randint(random_key_second, (3,), 0, N_TM)
    hit_marker = jnp.any(jnp.arange(N_TM)[:, None] == slab_groups_total[None, :], axis=1)
    factor = jax.random.uniform(random_key_third, shape, jnp.float32, 0.5, 0.8)
    rough_estimate = jnp.where(hit_marker[:, None, None, None], rough_estimate * factor, rough_estimate)
    return rough_estimate.astype(jnp.float32)


def draw_tile_ids(key, part):
    scores = jax.random.randint(key, (N_TM * INCREMENTS, N_SPACE, TILES_DEV), 0, 2 ** 18)
    scores = scores * TILES_DEV + jnp.arange(TILES_DEV, dtype=jnp.int32)
    unused_value, chosen = lax.top_k(scores, MAXT)
    return chosen.reshape(N_TM * INCREMENTS, N_SPACE * MAXT).astype(jnp.int32)


def draw_tile_count(key, part):
    key_one, random_key_second = jax.random.split(key)
    counts = jax.random.randint(key_one, (N_TM, INCREMENTS, N_SPACE), MAXT // 4, MAXT + 1)
    full_step = jax.random.randint(random_key_second, (N_TM, 1, N_SPACE), 0, INCREMENTS)
    counts = jnp.where(jnp.arange(INCREMENTS)[None, :, None] == full_step, MAXT, counts)
    return counts.reshape(N_TM * INCREMENTS, N_SPACE).astype(jnp.int32)


def block_scale(key, dims, pieces, low, high):
    factor_of = 1.0
    for axis_at, parts in pieces:
        heights = jax.random.uniform(jax.random.fold_in(jax.random.fold_in(key, 6), axis_at), (parts,), jnp.float32, low / len(pieces), high / len(pieces))
        factor_of = factor_of * jnp.repeat(jnp.exp(heights), dims[axis_at] // parts).reshape((-1,) + (1,) * (len(dims) - 1 - axis_at))
    return factor_of


def gaussian(stream_key, shape, deviation, most, pieces=(), kind=jnp.bfloat16):
    factor_of = block_scale(stream_key, shape, pieces, -0.22, 0.18) if pieces else 1.0
    array = jax.random.normal(stream_key, shape, jnp.float32) * deviation * factor_of
    return jnp.minimum(jnp.maximum(array, -most), most).astype(kind)


def setup_inputs(seed: int = 0) -> dict:
    arg_keys = jax.random.split(jax.random.key(seed), 8)
    return {
        "opening_guess_profile": gaussian(arg_keys[0], (N_TM, NX, NY, NZ), 1.0, 6.0, ((0, 32), (1, 16)), jnp.float32),
        "capacity": jnp.clip(jnp.exp(math.log(4.0) - 2.7725887 * jax.random.uniform(arg_keys[1], (NX, NY, NZ), jnp.float32) ** block_scale(arg_keys[1], (NX, NY, NZ), ((0, 16),), -0.2, 0.2)), 0.25, 4.0),
        "thermal_forcing": gaussian(arg_keys[2], (N_TM, NX, NY, NZ), 0.5, 3.0, ((0, 32), (1, 16)), jnp.float32),
        "rough_decay_factor": draw_rough_decay_factor(jax.random.fold_in(arg_keys[7], 71), 0),
        "tile_ids": draw_tile_ids(jax.random.fold_in(arg_keys[7], 71), 0),
        "tile_count": draw_tile_count(jax.random.fold_in(arg_keys[7], 71), 0),
        "tile_blocks": gaussian(arg_keys[6], (N_TM * INCREMENTS, N_SPACE * MAXT, TILE, TILE), 512 ** -0.5, 0.25, ((0, 32), (1, 16)), jnp.float32),
    }


COND = 1.0


def beside_sum(wide):
    center = wide[1:-1]
    padded = jnp.pad(center, ((0, 0), (1, 1), (1, 1)))
    total = wide[2:] + wide[:-2]
    total = total + padded[:, 2:, 1:-1] + padded[:, :-2, 1:-1]
    return total + padded[:, 1:-1, 2:] + padded[:, 1:-1, :-2]


def interface_fix(field, previous, tile_rows, live_count, blocks):
    shape = field.shape
    tile_len = blocks.shape[-1]
    delta = (field - previous).reshape(-1, tile_len)
    picked = delta[tile_rows]
    fixes = jnp.einsum("src,sc->sr", blocks, picked, precision=lax.Precision.HIGHEST)
    live = (jnp.arange(tile_rows.shape[0]) < live_count)[:, None]
    fixes = jnp.where(live, fixes, 0.0)
    tiles = field.reshape(-1, tile_len).at[tile_rows].add(fixes)
    return tiles.reshape(shape)


def slab_run(args):
    opening_moment, source, capacity, window_labels, window_tallies, window_partitions = args
    inverse = 1.0 / (capacity + 6.0 * COND)
    field = opening_moment
    for step_index in range(INCREMENTS):
        previous = field
        rhs = capacity * previous + source
        for sweep_index in range(SWEEPS):
            wide = jnp.pad(field, ((1, 1), (0, 0), (0, 0)))
            field = (rhs + COND * beside_sum(wide)) * inverse
        bricks = field.reshape(N_SPACE, -1, NY, NZ)
        old_bricks = previous.reshape(N_SPACE, -1, NY, NZ)
        rows = window_labels[step_index].reshape(N_SPACE, MAXT)
        counts = window_tallies[step_index]
        blocks = window_partitions[step_index].reshape(N_SPACE, MAXT, TILE, TILE)
        bricks = jax.vmap(interface_fix)(bricks, old_bricks, rows, counts, blocks)
        field = bricks.reshape(field.shape)
    return field


def reference(opening_guess_profile, capacity, thermal_forcing, rough_decay_factor, tile_ids, tile_count, tile_blocks):
    window_labels = tile_ids.reshape(N_TM, INCREMENTS, -1)
    window_tallies = tile_count.reshape(N_TM, INCREMENTS, -1)
    window_partitions = tile_blocks.reshape(N_TM, INCREMENTS, -1, TILE, TILE)

    def lone_window(args):
        opening_moment, source, slab_id, slab_count, slab_block = args
        return slab_run((opening_moment, source, capacity, slab_id, slab_count, slab_block))

    accurate_ending_thermal_state = lax.map(lone_window, (opening_guess_profile, thermal_forcing, window_labels, window_tallies, window_partitions))

    def propagation_sequence(carry, items):
        index, opening_moment, ending, rough_estimate = items
        first = index == 0
        current = jnp.where(first, opening_moment, carry)
        following = jnp.where(first, ending, rough_estimate * (carry - opening_moment) + ending)
        return following, current

    position_numbers = jnp.arange(N_TM).astype(jnp.int32)
    unused_value, updated_opening_state = lax.scan(propagation_sequence, jnp.zeros_like(opening_guess_profile[0]), (position_numbers, opening_guess_profile, accurate_ending_thermal_state, rough_decay_factor))
    return updated_opening_state, accurate_ending_thermal_state
```

```python
import jax
import jax.numpy as jnp
from jax import lax
from jax.experimental import pallas as pl
from jax.experimental.pallas import tpu as pltpu
from jax.sharding import Mesh
from jax.sharding import PartitionSpec as P

INCREMENTS = 8
SWEEPS = 4
TM = ("tm_0", "tm_1", "tm_2")
SPACE = ("sx", "sz")
MESH = pl.DeviceIdType.MESH
COND = 1.0

NZD = 4
NXD = 4
DEEP = 4
LAYERS = DEEP * NZD
ROWS = 32
NY = ROWS * NZD
NZ = 256
TILE = 64
MAXT = 8
PAIRS = MAXT // 2


def nothing_yet(x, identity):
    return jax.tree.map(
        lambda a, e: jnp.broadcast_to(jnp.asarray(e, a.dtype), a.shape), x, identity
    )


def carried_in(x, axes, combine, identity):
    before = start = nothing_yet(x, identity)
    total = x
    for axis in reversed(axes):
        length, position = (lax.axis_size(axis), lax.axis_index(axis))
        pieces = jax.tree.map(lambda part: lax.all_gather(part, axis), total)
        inside, total = (start, start)
        for k in range(length):
            passed = k < position
            total = combine(total, jax.tree.map(lambda part: part[k], pieces))
            inside = jax.tree.map(lambda new, old: jnp.where(passed, new, old), total, inside)
        before = combine(inside, before)
    return before


def fine_kernel(
    g_ref, c_ref, f_ref, ids_ref, cnt_ref, m_ref,
    e_ref,
    p, a, b, inv, cap, src, rhs, back,
    xlo, xhi, zlo, zhi, zs_lo, zs_hi, inv_lo, inv_hi,
    bt, idv, dx, ids_s,
    in_send, in_recv, id_send, id_recv, h_send, h_recv, b_send, b_recv, o_send, o_recv, loc,
):
    sx = lax.axis_index("sx")
    sz = lax.axis_index("sz")
    has_xl, has_xr = sx > 0, sx < NXD - 1
    has_zl, has_zr = sz > 0, sz < NZD - 1

    barrier = pltpu.get_barrier_semaphore()
    for o in range(1, NZD):
        pl.semaphore_signal(
            barrier, inc=1, device_id={"sz": lax.rem(sz + o, NZD)}, device_id_type=MESH
        )

    @pl.when(has_xl)
    def _():
        pl.semaphore_signal(barrier, inc=1, device_id={"sx": sx - 1}, device_id_type=MESH)

    @pl.when(has_xr)
    def _():
        pl.semaphore_signal(barrier, inc=1, device_id={"sx": sx + 1}, device_id_type=MESH)

    idv[sz] = jnp.zeros((INCREMENTS, 128), jnp.int32)
    idv[sz, :, 0:MAXT] = ids_ref[...]
    idv[sz, :, MAXT : MAXT + 1] = cnt_ref[...]
    for k in range(INCREMENTS):
        for i in range(PAIRS):
            two = m_ref[k, 2 * i : 2 * i + 2].reshape(2 * TILE, TILE)
            bt[k, sz, i] = two.T
    zero_x = jnp.zeros((2, ROWS, NZ), jnp.float32)
    zero_z = jnp.zeros((2, LAYERS, NZ), jnp.float32)

    @pl.when(jnp.logical_not(has_xl))
    def _():
        xlo[...] = zero_x

    @pl.when(jnp.logical_not(has_xr))
    def _():
        xhi[...] = zero_x

    @pl.when(jnp.logical_not(has_zl))
    def _():
        zlo[...] = zero_z

    @pl.when(jnp.logical_not(has_zr))
    def _():
        zhi[...] = zero_z

    pl.semaphore_wait(
        barrier, NZD - 1 + has_xl.astype(jnp.int32) + has_xr.astype(jnp.int32)
    )

    def dealt(n, o):
        to = lax.rem(sz + o, NZD)
        source = (g_ref.at[0], f_ref.at[0], c_ref)[n]
        target = (p, src, cap)[n]
        return pltpu.make_async_remote_copy(
            src_ref=source.at[:, pl.ds(ROWS * to, ROWS), :],
            dst_ref=target.at[pl.ds(DEEP * sz, DEEP)],
            send_sem=in_send.at[n, o],
            recv_sem=in_recv.at[n, o],
            device_id={"sz": to},
            device_id_type=MESH,
        )

    def listed(o):
        to = lax.rem(sz + o, NZD)
        return pltpu.make_async_remote_copy(
            src_ref=idv.at[sz],
            dst_ref=idv.at[sz],
            send_sem=id_send.at[o],
            recv_sem=id_recv.at[o],
            device_id={"sz": to},
            device_id_type=MESH,
        )

    for o in range(1, NZD):
        listed(o).start()
    for n in range(3):
        for o in range(1, NZD):
            dealt(n, o).start()

    def block_copy(k, d, r):
        brick = sz - r if d == 0 else sz + r
        return pltpu.make_async_remote_copy(
            src_ref=bt.at[k, jnp.clip(brick, 0, NZD - 1)],
            dst_ref=bt.at[k, jnp.clip(brick, 0, NZD - 1)],
            send_sem=b_send.at[lax.rem(k, 2), d, r],
            recv_sem=b_recv.at[lax.rem(k, 2), d, r],
            device_id={"sz": jnp.clip(sz + 1 if d == 0 else sz - 1, 0, NZD - 1)},
            device_id_type=MESH,
        )

    def block_start(k, r):
        @pl.when(jnp.logical_and(sz - r >= 0, has_zr))
        def _():
            block_copy(k, 0, r).start()

        @pl.when(jnp.logical_and(sz + r < NZD, has_zl))
        def _():
            block_copy(k, 1, r).start()

    def block_wait(k, r):
        @pl.when(jnp.logical_and(sz - r >= 0, has_zr))
        def _():
            block_copy(k, 0, r).wait_send()

        @pl.when(jnp.logical_and(sz + r < NZD, has_zl))
        def _():
            block_copy(k, 1, r).wait_send()

        @pl.when(sz - 1 - r >= 0)
        def _():
            block_copy(k, 0, r).wait_recv()

        @pl.when(sz + 1 + r < NZD)
        def _():
            block_copy(k, 1, r).wait_recv()

    block_start(0, 0)
    mine = pl.ds(DEEP * sz, DEEP)
    p[mine] = g_ref[0, :, pl.ds(ROWS * sz, ROWS), :]
    src[mine] = f_ref[0, :, pl.ds(ROWS * sz, ROWS), :]
    cap[mine] = c_ref[:, pl.ds(ROWS * sz, ROWS), :]
    for o in range(1, NZD):
        listed(o).wait()
    lists = pltpu.make_async_copy(idv, ids_s, loc)
    lists.start()
    for n in range(3):
        for o in range(1, NZD):
            dealt(n, o).wait()
    lists.wait()
    block_wait(0, 0)
    block_start(0, 1)

    for l in range(LAYERS):
        inv[l] = 1.0 / (cap[l] + 6.0 * COND)
    inv_lo[...] = inv[:, 0, :]
    inv_hi[...] = inv[:, ROWS - 1, :]
    zs_lo[0] = p[:, 0, :]
    zs_hi[0] = p[:, ROWS - 1, :]

    row = lax.broadcasted_iota(jnp.int32, (ROWS, NZ), 0)
    lane = lax.broadcasted_iota(jnp.int32, (ROWS, NZ), 1)

    def halo(field, slot):
        def copy(n, source, target, where):
            return pltpu.make_async_remote_copy(
                src_ref=source,
                dst_ref=target,
                send_sem=h_send.at[n, slot],
                recv_sem=h_recv.at[n, slot],
                device_id=where,
                device_id_type=MESH,
            )

        xl, xr = {"sx": jnp.maximum(sx - 1, 0)}, {"sx": jnp.minimum(sx + 1, NXD - 1)}
        zl, zr = {"sz": jnp.maximum(sz - 1, 0)}, {"sz": jnp.minimum(sz + 1, NZD - 1)}
        return (
            (has_xl, has_xr, lambda: copy(0, field.at[0], xhi.at[slot], xl)),
            (has_xr, has_xl, lambda: copy(1, field.at[LAYERS - 1], xlo.at[slot], xr)),
            (has_zl, has_zr, lambda: copy(2, zs_lo.at[slot], zhi.at[slot], zl)),
            (has_zr, has_zl, lambda: copy(3, zs_hi.at[slot], zlo.at[slot], zr)),
        )

    def sweep(old, new, slot, first, last, between):
        copies = halo(old, slot)
        for sends, unused, copy in copies:
            @pl.when(sends)
            def _(copy=copy):
                copy().start()

        between()
        for l in range(LAYERS):
            w = old[l]
            t = jnp.where(row == 0, 0.0, pltpu.roll(w, 1, 0))
            t = t + jnp.where(row == ROWS - 1, 0.0, pltpu.roll(w, ROWS - 1, 0))
            t = t + jnp.where(lane == 0, 0.0, pltpu.roll(w, 1, 1))
            t = t + jnp.where(lane == NZ - 1, 0.0, pltpu.roll(w, NZ - 1, 1))
            if l > 0:
                t = t + old[l - 1]
            if l < LAYERS - 1:
                t = t + old[l + 1]
            if first:
                r = cap[l] * w + src[l]
                rhs[l] = r
            else:
                r = rhs[l]
            new[l] = (r + COND * t) * inv[l]
        for sends, gets, copy in copies:
            @pl.when(sends)
            def _(copy=copy):
                copy().wait_send()

            @pl.when(gets)
            def _(copy=copy):
                copy().wait_recv()

        new[0] = new[0] + COND * (inv[0] * xlo[slot])
        new[LAYERS - 1] = new[LAYERS - 1] + COND * (inv[LAYERS - 1] * xhi[slot])
        lo = new[:, 0, :] + COND * (inv_lo[...] * zlo[slot])
        hi = new[:, ROWS - 1, :] + COND * (inv_hi[...] * zhi[slot])
        new[:, 0, :] = lo
        new[:, ROWS - 1, :] = hi
        if not last:
            zs_lo[1 - slot] = lo
            zs_hi[1 - slot] = hi

    lane_r = lax.broadcasted_iota(jnp.int32, (1, 128), 1) < TILE
    lane_c = lax.broadcasted_iota(jnp.int32, (TILE, 128), 1) < TILE
    cell = lax.broadcasted_iota(jnp.int32, (DEEP * ROWS, NZ), 0)

    def fix(k):
        places = []
        for brick in range(NZD):
            count = ids_s[brick, k, MAXT]
            for i in range(PAIRS):
                halves = []
                for odd in range(2):
                    slot = 2 * i + odd
                    tile = ids_s[brick, k, slot]
                    quad = lax.rem(tile, 4)
                    line = lax.rem(tile // 4, NY) - ROWS * sz
                    layer = tile // (4 * NY)
                    owned = (line >= 0) & (line < ROWS) & (slot < count)
                    line_in = jnp.clip(line, 0, ROWS - 1)
                    where = DEEP * brick + layer
                    d = b[where, pl.ds(line_in, 1), :] - p[where, pl.ds(line_in, 1), :]
                    h = jnp.where(quad >= 2, d[:, 128:], d[:, :128])
                    turn = lax.rem(quad, 2) != odd
                    h = jnp.where(turn, pltpu.roll(h, TILE, 1), h)
                    halves.append(h)
                    places.append((jnp.where(owned, layer * ROWS + line_in, -1), quad, turn))
                dx[brick * PAIRS + i : brick * PAIRS + i + 1, :] = jnp.where(
                    lane_r, halves[0], halves[1]
                )
        columns = dx[...].T
        for brick in range(NZD):
            total = b[DEEP * brick : DEEP * (brick + 1)].reshape(DEEP * ROWS, NZ)
            for i in range(PAIRS):
                at = brick * PAIRS + i
                d = jnp.where(
                    lane_c,
                    jnp.broadcast_to(columns[0:TILE, at : at + 1], (TILE, 128)),
                    jnp.broadcast_to(columns[TILE : 2 * TILE, at : at + 1], (TILE, 128)),
                )
                sums = jnp.sum(bt[k, brick, i] * d, axis=0, keepdims=True)
                for odd in range(2):
                    place, quad, turn = places[brick * MAXT + 2 * i + odd]
                    h = jnp.where(turn, pltpu.roll(sums, TILE, 1), sums)
                    right = lax.rem(quad, 2) == 1
                    h = jnp.where(lane_r != right, h, 0.0)
                    wide = jnp.concatenate(
                        [jnp.where(quad < 2, h, 0.0), jnp.where(quad < 2, 0.0, h)], axis=1
                    )
                    total = total + jnp.where(cell == place, wide, 0.0)
            p[DEEP * brick : DEEP * (brick + 1)] = total.reshape(DEEP, ROWS, NZ)
        zs_lo[0] = p[:, 0, :]
        zs_hi[0] = p[:, ROWS - 1, :]

    dx[...] = jnp.zeros((128, 128), jnp.float32)

    def step(k, carry):
        def one():
            block_wait(k, 1)
            block_start(k, 2)

        def three():
            @pl.when(k < INCREMENTS - 1)
            def _():
                block_start(k + 1, 0)

        def four():
            @pl.when(k < INCREMENTS - 1)
            def _():
                block_wait(k + 1, 0)
                block_start(k + 1, 1)

        sweep(p, a, 0, True, False, one)
        sweep(a, b, 1, False, False, lambda: None)
        sweep(b, a, 0, False, False, three)
        sweep(a, b, 1, False, True, four)
        block_wait(k, 2)
        fix(k)
        return carry

    lax.fori_loop(0, INCREMENTS, step, 0)

    def returned(o):
        to = lax.rem(sz + o, NZD)
        return pltpu.make_async_remote_copy(
            src_ref=p.at[pl.ds(DEEP * to, DEEP)],
            dst_ref=back.at[:, pl.ds(ROWS * sz, ROWS), :],
            send_sem=o_send.at[o],
            recv_sem=o_recv.at[o],
            device_id={"sz": to},
            device_id_type=MESH,
        )

    for o in range(1, NZD):
        returned(o).start()
    back[:, pl.ds(ROWS * sz, ROWS), :] = p[mine]
    for o in range(1, NZD):
        returned(o).wait()
    e_ref[0] = back[...]


def fine(g, c, f, ids, cnt, m):
    vm = pl.BlockSpec(memory_space=pltpu.VMEM)
    field = pltpu.VMEM((LAYERS, ROWS, NZ), jnp.float32)
    xf = pltpu.VMEM((2, ROWS, NZ), jnp.float32)
    zf = pltpu.VMEM((2, LAYERS, NZ), jnp.float32)
    z1 = pltpu.VMEM((LAYERS, NZ), jnp.float32)
    dma = pltpu.SemaphoreType.DMA
    return pl.pallas_call(
        fine_kernel,
        out_shape=jax.ShapeDtypeStruct(g.shape, jnp.float32),
        in_specs=[vm] * 6,
        out_specs=vm,
        scratch_shapes=[field] * 7
        + [pltpu.VMEM((DEEP, NY, NZ), jnp.float32)]
        + [xf, xf, zf, zf, zf, zf, z1, z1]
        + [
            pltpu.VMEM((INCREMENTS, NZD, PAIRS, TILE, 128), jnp.float32),
            pltpu.VMEM((NZD, INCREMENTS, 128), jnp.int32),
            pltpu.VMEM((128, 128), jnp.float32),
            pltpu.SMEM((NZD, INCREMENTS, 128), jnp.int32),
            dma((3, NZD)), dma((3, NZD)), dma((NZD,)), dma((NZD,)),
            dma((4, 2)), dma((4, 2)), dma((2, 2, 3)), dma((2, 2, 3)),
            dma((NZD,)), dma((NZD,)), dma,
        ],
        compiler_params=pltpu.CompilerParams(
            collective_id=0, has_side_effects=True, vmem_limit_bytes=48 << 20
        ),
    )(g, c, f, ids, cnt, m)


def shards(
    opening_guess_profile,
    capacity,
    thermal_forcing,
    rough_decay_factor,
    tile_ids,
    tile_count,
    tile_blocks,
):
    opening_moment = opening_guess_profile[0]
    rough_estimate = rough_decay_factor[0]
    accurate_ending_thermal_state = fine(
        opening_guess_profile, capacity, thermal_forcing, tile_ids, tile_count, tile_blocks
    )[0]
    opening_window = lax.axis_index(TM) == 0
    own_scale = jnp.where(opening_window, 0.0, rough_estimate)
    own_shift = jnp.where(
        opening_window,
        accurate_ending_thermal_state,
        accurate_ending_thermal_state - rough_estimate * opening_moment,
    )

    def compose(prior_iterate, later):
        return (later[0] * prior_iterate[0], later[0] * prior_iterate[1] + later[1])

    scale, shift = carried_in(
        (own_scale, own_shift),
        TM,
        compose,
        (jnp.ones_like(rough_estimate), jnp.zeros_like(rough_estimate)),
    )
    updated_opening_state = scale * opening_moment + shift
    return (updated_opening_state[None], accurate_ending_thermal_state[None])


def solution(mesh):
    split = Mesh(
        mesh.devices.reshape(8, 2, 2, NXD, NZD), ("tm_0", "tm_1", "tm_2", "sx", "sz")
    )
    return jax.shard_map(
        shards,
        mesh=split,
        in_specs=(
            P(TM, SPACE, None, None),
            P(SPACE, None, None),
            P(TM, SPACE, None, None),
            P(TM, SPACE, None, None),
            P(TM, SPACE),
            P(TM, SPACE),
            P(TM, SPACE, None, None),
        ),
        out_specs=(P(TM, SPACE, None, None), P(TM, SPACE, None, None)),
        check_vma=False,
    )
```

```python
import jax
import jax.numpy as jnp
from jax import lax
from jax.experimental import pallas as pl
from jax.experimental.pallas import tpu as pltpu
from jax.sharding import Mesh
from jax.sharding import PartitionSpec as P

INCREMENTS = 8
SWEEPS = 4
TM = ("tm_0", "tm_1", "tm_2")
SPACE = ("sx", "sz")
MESH = pl.DeviceIdType.MESH
COND = 1.0

NZD = 4
NXD = 4
NYD = 8
DEEP = 4
LAYERS = DEEP * NZD
HALF = LAYERS // 2
ROWS = 32
NY = ROWS * NZD
NZ = 256
TILE = 64
MAXT = 8
PAIRS = MAXT // 2


def fine_kernel(
    g_ref, c_ref, f_ref, d_ref, ids_ref, cnt_ref, m_ref,
    x_ref, e_ref,
    p, a, b, inv, cap, src, rhs, dec, gp, back, xback,
    xlo, xhi, zlo, zhi, zs_lo, zs_hi, inv_lo, inv_hi,
    bt, idv, dx,
    do, go, eo, a0, a1, ga0, ga1, ac, ao, ay, b0, bc, bo, pin, pout, x0, x1,
    ids_s,
    in_send, in_recv, id_send, id_recv, h_send, h_recv, b_send, b_recv, o_send, o_recv, loc,
    cs_send, cs_recv, a_send, a_recv, z_send, z_recv, y_send, y_recv, x_send, x_recv,
):
    sx = lax.axis_index("sx")
    sz = lax.axis_index("sz")
    y = lax.axis_index("tm_0")
    zh = lax.axis_index("tm_1")
    core = lax.axis_index("tm_2")
    dz = 1 - 2 * zh
    q = (NZD - 1) * zh + dz * sz

    def quarter(device):
        return (NZD - 1) * zh + dz * device

    has_xl, has_xr = sx > 0, sx < NXD - 1
    has_bl, has_br = sz > 0, sz < NZD - 1
    has_zl, has_zr = q > 0, q < NZD - 1
    has_yl, has_yr = y > 0, y < NYD - 1
    across = {"tm_1": 1 - zh, "sz": NZD - 1 - sz}
    beside = {"tm_2": 1 - core}

    barrier = pltpu.get_barrier_semaphore()
    for o in range(1, NZD):
        pl.semaphore_signal(
            barrier, inc=1, device_id={"sz": lax.rem(sz + o, NZD)}, device_id_type=MESH
        )
    for t in range(NZD):
        pl.semaphore_signal(
            barrier, inc=1, device_id={"tm_2": 1 - core, "sz": t}, device_id_type=MESH
        )
    pl.semaphore_signal(barrier, inc=1, device_id=across, device_id_type=MESH)

    @pl.when(has_yl)
    def _():
        pl.semaphore_signal(barrier, inc=1, device_id={"tm_0": y - 1}, device_id_type=MESH)

    @pl.when(has_yr)
    def _():
        pl.semaphore_signal(barrier, inc=1, device_id={"tm_0": y + 1}, device_id_type=MESH)

    @pl.when(has_xl)
    def _():
        pl.semaphore_signal(barrier, inc=1, device_id={"sx": sx - 1}, device_id_type=MESH)

    @pl.when(has_xr)
    def _():
        pl.semaphore_signal(barrier, inc=1, device_id={"sx": sx + 1}, device_id_type=MESH)

    idv[sz] = jnp.zeros((INCREMENTS, 128), jnp.int32)
    idv[sz, :, 0:MAXT] = ids_ref[...]
    idv[sz, :, MAXT : MAXT + 1] = cnt_ref[...]
    for k in range(INCREMENTS):
        for i in range(PAIRS):
            two = m_ref[k, 2 * i : 2 * i + 2].reshape(2 * TILE, TILE)
            bt[k, sz, i] = two.T
    zero_x = jnp.zeros((2, ROWS, NZ), jnp.float32)
    zero_z = jnp.zeros((2, LAYERS, NZ), jnp.float32)

    @pl.when(jnp.logical_not(has_xl))
    def _():
        xlo[...] = zero_x

    @pl.when(jnp.logical_not(has_xr))
    def _():
        xhi[...] = zero_x

    @pl.when(jnp.logical_not(has_zl))
    def _():
        zlo[...] = zero_z

    @pl.when(jnp.logical_not(has_zr))
    def _():
        zhi[...] = zero_z

    pl.semaphore_wait(
        barrier,
        2 * NZD
        + has_xl.astype(jnp.int32) + has_xr.astype(jnp.int32)
        + has_yl.astype(jnp.int32) + has_yr.astype(jnp.int32),
    )

    def dealt(n, o):
        to = lax.rem(sz + o, NZD)
        source = (g_ref.at[0], f_ref.at[0], c_ref, d_ref.at[0])[n]
        target = (p, src, cap, dec)[n]
        return pltpu.make_async_remote_copy(
            src_ref=source.at[:, pl.ds(ROWS * quarter(to), ROWS), :],
            dst_ref=target.at[pl.ds(DEEP * sz, DEEP)],
            send_sem=in_send.at[n, o],
            recv_sem=in_recv.at[n, o],
            device_id={"sz": to},
            device_id_type=MESH,
        )

    def listed(o):
        to = lax.rem(sz + o, NZD)
        return pltpu.make_async_remote_copy(
            src_ref=idv.at[sz],
            dst_ref=idv.at[sz],
            send_sem=id_send.at[o],
            recv_sem=id_recv.at[o],
            device_id={"sz": to},
            device_id_type=MESH,
        )

    for o in range(1, NZD):
        listed(o).start()
    for n in range(3):
        for o in range(1, NZD):
            dealt(n, o).start()

    def block_copy(k, d, r):
        brick = sz - r if d == 0 else sz + r
        return pltpu.make_async_remote_copy(
            src_ref=bt.at[k, jnp.clip(brick, 0, NZD - 1)],
            dst_ref=bt.at[k, jnp.clip(brick, 0, NZD - 1)],
            send_sem=b_send.at[lax.rem(k, 2), d, r],
            recv_sem=b_recv.at[lax.rem(k, 2), d, r],
            device_id={"sz": jnp.clip(sz + 1 if d == 0 else sz - 1, 0, NZD - 1)},
            device_id_type=MESH,
        )

    def block_start(k, r):
        @pl.when(jnp.logical_and(sz - r >= 0, has_br))
        def _():
            block_copy(k, 0, r).start()

        @pl.when(jnp.logical_and(sz + r < NZD, has_bl))
        def _():
            block_copy(k, 1, r).start()

    def block_wait(k, r):
        @pl.when(jnp.logical_and(sz - r >= 0, has_br))
        def _():
            block_copy(k, 0, r).wait_send()

        @pl.when(jnp.logical_and(sz + r < NZD, has_bl))
        def _():
            block_copy(k, 1, r).wait_send()

        @pl.when(sz - 1 - r >= 0)
        def _():
            block_copy(k, 0, r).wait_recv()

        @pl.when(sz + 1 + r < NZD)
        def _():
            block_copy(k, 1, r).wait_recv()

    block_start(0, 0)
    mine = pl.ds(DEEP * sz, DEEP)
    own_rows = pl.ds(ROWS * q, ROWS)
    p[mine] = g_ref[0, :, own_rows, :]
    src[mine] = f_ref[0, :, own_rows, :]
    cap[mine] = c_ref[:, own_rows, :]
    dec[mine] = d_ref[0, :, own_rows, :]
    for o in range(1, NZD):
        listed(o).wait()
    lists = pltpu.make_async_copy(idv, ids_s, loc)
    lists.start()
    for n in range(3):
        for o in range(1, NZD):
            dealt(n, o).wait()
    lists.wait()
    block_wait(0, 0)
    block_start(0, 1)

    for l in range(LAYERS):
        inv[l] = 1.0 / (cap[l] + 6.0 * COND)
        gp[l] = p[l]
    inv_lo[...] = inv[:, 0, :]
    inv_hi[...] = inv[:, ROWS - 1, :]
    zs_lo[0] = p[:, 0, :]
    zs_hi[0] = p[:, ROWS - 1, :]

    row = lax.broadcasted_iota(jnp.int32, (ROWS, NZ), 0)
    lane = lax.broadcasted_iota(jnp.int32, (ROWS, NZ), 1)

    def halo(field, slot):
        def copy(n, source, target, where):
            return pltpu.make_async_remote_copy(
                src_ref=source,
                dst_ref=target,
                send_sem=h_send.at[n, slot],
                recv_sem=h_recv.at[n, slot],
                device_id=where,
                device_id_type=MESH,
            )

        xl, xr = {"sx": jnp.maximum(sx - 1, 0)}, {"sx": jnp.minimum(sx + 1, NXD - 1)}
        zl = {"sz": jnp.clip(sz - dz, 0, NZD - 1)}
        zr = {"sz": jnp.clip(sz + dz, 0, NZD - 1)}
        return (
            (has_xl, has_xr, lambda: copy(0, field.at[0], xhi.at[slot], xl)),
            (has_xr, has_xl, lambda: copy(1, field.at[LAYERS - 1], xlo.at[slot], xr)),
            (has_zl, has_zr, lambda: copy(2, zs_lo.at[slot], zhi.at[slot], zl)),
            (has_zr, has_zl, lambda: copy(3, zs_hi.at[slot], zlo.at[slot], zr)),
        )

    def sweep(old, new, slot, first, last, between):
        copies = halo(old, slot)
        for sends, unused, copy in copies:
            @pl.when(sends)
            def _(copy=copy):
                copy().start()

        between()
        for l in range(LAYERS):
            w = old[l]
            t = jnp.where(row == 0, 0.0, pltpu.roll(w, 1, 0))
            t = t + jnp.where(row == ROWS - 1, 0.0, pltpu.roll(w, ROWS - 1, 0))
            t = t + jnp.where(lane == 0, 0.0, pltpu.roll(w, 1, 1))
            t = t + jnp.where(lane == NZ - 1, 0.0, pltpu.roll(w, NZ - 1, 1))
            if l > 0:
                t = t + old[l - 1]
            if l < LAYERS - 1:
                t = t + old[l + 1]
            if first:
                r = cap[l] * w + src[l]
                rhs[l] = r
            else:
                r = rhs[l]
            new[l] = (r + COND * t) * inv[l]
        for sends, gets, copy in copies:
            @pl.when(sends)
            def _(copy=copy):
                copy().wait_send()

            @pl.when(gets)
            def _(copy=copy):
                copy().wait_recv()

        new[0] = new[0] + COND * (inv[0] * xlo[slot])
        new[LAYERS - 1] = new[LAYERS - 1] + COND * (inv[LAYERS - 1] * xhi[slot])
        lo = new[:, 0, :] + COND * (inv_lo[...] * zlo[slot])
        hi = new[:, ROWS - 1, :] + COND * (inv_hi[...] * zhi[slot])
        new[:, 0, :] = lo
        new[:, ROWS - 1, :] = hi
        if not last:
            zs_lo[1 - slot] = lo
            zs_hi[1 - slot] = hi

    lane_r = lax.broadcasted_iota(jnp.int32, (1, 128), 1) < TILE
    lane_c = lax.broadcasted_iota(jnp.int32, (TILE, 128), 1) < TILE
    cell = lax.broadcasted_iota(jnp.int32, (DEEP * ROWS, NZ), 0)

    def fix(k):
        places = []
        for brick in range(NZD):
            count = ids_s[brick, k, MAXT]
            for i in range(PAIRS):
                halves = []
                for odd in range(2):
                    slot = 2 * i + odd
                    tile = ids_s[brick, k, slot]
                    quad = lax.rem(tile, 4)
                    line = lax.rem(tile // 4, NY) - ROWS * q
                    layer = tile // (4 * NY)
                    owned = (line >= 0) & (line < ROWS) & (slot < count)
                    line_in = jnp.clip(line, 0, ROWS - 1)
                    where = DEEP * brick + layer
                    d = b[where, pl.ds(line_in, 1), :] - p[where, pl.ds(line_in, 1), :]
                    h = jnp.where(quad >= 2, d[:, 128:], d[:, :128])
                    turn = lax.rem(quad, 2) != odd
                    h = jnp.where(turn, pltpu.roll(h, TILE, 1), h)
                    halves.append(h)
                    places.append((jnp.where(owned, layer * ROWS + line_in, -1), quad, turn))
                dx[brick * PAIRS + i : brick * PAIRS + i + 1, :] = jnp.where(
                    lane_r, halves[0], halves[1]
                )
        columns = dx[...].T
        for brick in range(NZD):
            total = b[DEEP * brick : DEEP * (brick + 1)].reshape(DEEP * ROWS, NZ)
            for i in range(PAIRS):
                at = brick * PAIRS + i
                d = jnp.where(
                    lane_c,
                    jnp.broadcast_to(columns[0:TILE, at : at + 1], (TILE, 128)),
                    jnp.broadcast_to(columns[TILE : 2 * TILE, at : at + 1], (TILE, 128)),
                )
                sums = jnp.sum(bt[k, brick, i] * d, axis=0, keepdims=True)
                for odd in range(2):
                    place, quad, turn = places[brick * MAXT + 2 * i + odd]
                    h = jnp.where(turn, pltpu.roll(sums, TILE, 1), sums)
                    right = lax.rem(quad, 2) == 1
                    h = jnp.where(lane_r != right, h, 0.0)
                    wide = jnp.concatenate(
                        [jnp.where(quad < 2, h, 0.0), jnp.where(quad < 2, 0.0, h)], axis=1
                    )
                    total = total + jnp.where(cell == place, wide, 0.0)
            p[DEEP * brick : DEEP * (brick + 1)] = total.reshape(DEEP, ROWS, NZ)
        zs_lo[0] = p[:, 0, :]
        zs_hi[0] = p[:, ROWS - 1, :]

    dx[...] = jnp.zeros((128, 128), jnp.float32)

    half = pl.ds(HALF * core, HALF)
    rest = pl.ds(HALF * (1 - core), HALF)
    first_slab = jnp.logical_and(y == 0, zh == 0)

    def swapped(n, source, target):
        return pltpu.make_async_remote_copy(
            src_ref=source.at[rest],
            dst_ref=target,
            send_sem=cs_send.at[n],
            recv_sem=cs_recv.at[n],
            device_id=beside,
            device_id_type=MESH,
        )

    def factors(n):
        return swapped(n, (dec, gp)[n], (do, go)[n])

    def factors_ready():
        for i in range(HALF):
            own_d, own_g = dec[HALF * core + i], gp[HALF * core + i]
            d0 = jnp.where(core == 0, own_d, do[i])
            d1 = jnp.where(core == 0, do[i], own_d)
            g0 = jnp.where(core == 0, own_g, go[i])
            g1 = jnp.where(core == 0, go[i], own_g)
            d0 = jnp.where(first_slab, 0.0, d0)
            a0[i] = d0
            a1[i] = d1
            ga0[i] = d0 * g0
            ga1[i] = d1 * g1
            ac[i] = d0 * d1
            pout[i] = g0

    def scales():
        return pltpu.make_async_remote_copy(
            src_ref=ac,
            dst_ref=ao,
            send_sem=a_send,
            recv_sem=a_recv,
            device_id=across,
            device_id_type=MESH,
        )

    def shift(i):
        return pltpu.make_async_remote_copy(
            src_ref=bc.at[i],
            dst_ref=bo.at[i],
            send_sem=z_send.at[i],
            recv_sem=z_recv.at[i],
            device_id=across,
            device_id_type=MESH,
        )

    def state(i):
        return pltpu.make_async_remote_copy(
            src_ref=pout.at[i],
            dst_ref=pin.at[i],
            send_sem=y_send.at[i],
            recv_sem=y_recv.at[i],
            device_id={"tm_0": jnp.minimum(y + 1, NYD - 1)},
            device_id_type=MESH,
        )

    def step(k, carry):
        def one():
            block_wait(k, 1)
            block_start(k, 2)

        def two():
            for o in range(1, NZD):
                @pl.when(k == o - 1)
                def _(o=o):
                    dealt(3, o).start()

            @pl.when(k == 3)
            def _():
                for o in range(1, NZD):
                    dealt(3, o).wait()
                factors(0).start()
                factors(1).start()

            @pl.when(k == 4)
            def _():
                factors(0).wait()
                factors(1).wait()
                factors_ready()
                scales().start()

            @pl.when(k == 5)
            def _():
                scales().wait()
                for i in range(HALF):
                    ay[i] = ac[i] * ao[i]

        def three():
            @pl.when(k < INCREMENTS - 1)
            def _():
                block_start(k + 1, 0)

        def four():
            @pl.when(k < INCREMENTS - 1)
            def _():
                block_wait(k + 1, 0)
                block_start(k + 1, 1)

        sweep(p, a, 0, True, False, one)
        sweep(a, b, 1, False, False, two)
        sweep(b, a, 0, False, False, three)
        sweep(a, b, 1, False, True, four)
        block_wait(k, 2)
        fix(k)
        return carry

    lax.fori_loop(0, INCREMENTS, step, 0)

    def returned(o):
        to = lax.rem(sz + o, NZD)
        return pltpu.make_async_remote_copy(
            src_ref=p.at[pl.ds(DEEP * to, DEEP)],
            dst_ref=back.at[:, own_rows, :],
            send_sem=o_send.at[o],
            recv_sem=o_recv.at[o],
            device_id={"sz": to},
            device_id_type=MESH,
        )

    swapped(2, p, eo).start()
    swapped(2, p, eo).wait()
    for i in range(HALF):
        own = p[HALF * core + i]
        s0 = jnp.where(core == 0, own, eo[i]) - ga0[i]
        s1 = jnp.where(core == 0, eo[i], own) - ga1[i]
        b0[i] = s0
        bc[i] = a1[i] * s0 + s1
        shift(i).start()
    for o in range(1, NZD):
        returned(o).start()
    back[:, own_rows, :] = p[mine]

    def sent(slab, part, source):
        return pltpu.make_async_remote_copy(
            src_ref=(x0, x1)[slab].at[pl.ds(DEEP * part, DEEP)],
            dst_ref=xback.at[:, pl.ds(ROWS * quarter(source), ROWS), :],
            send_sem=x_send.at[slab, part],
            recv_sem=x_recv.at[source],
            device_id={"tm_2": slab, "sz": 2 * core + part},
            device_id_type=MESH,
        )

    def stays(slab, part):
        return jnp.logical_and(core == slab, sz == 2 * core + part)

    for i in range(HALF):
        shift(i).wait()

        @pl.when(has_yl)
        def _(i=i):
            state(i).wait_recv()
            before = pin[i]
            pout[i] = before

        before = pout[i]
        shift_0 = jnp.where(zh == 0, bc[i], bo[i])
        shift_1 = jnp.where(zh == 0, bo[i], bc[i])
        scale_0 = jnp.where(zh == 0, ac[i], ao[i])
        scale_1 = jnp.where(zh == 0, ao[i], ac[i])
        pout[i] = ay[i] * before + (scale_1 * shift_0 + shift_1)

        @pl.when(has_yr)
        def _(i=i):
            state(i).start()

        start = jnp.where(zh == 0, before, scale_0 * before + shift_0)
        x0[i] = start
        x1[i] = a0[i] * start + b0[i]
        if i % DEEP == DEEP - 1:
            part = i // DEEP
            for slab in range(2):
                @pl.when(jnp.logical_not(stays(slab, part)))
                def _(slab=slab, part=part):
                    sent(slab, part, sz).start()

                @pl.when(stays(slab, part))
                def _(slab=slab, part=part):
                    xback[:, own_rows, :] = (x0, x1)[slab][DEEP * part : DEEP * (part + 1)]

    for o in range(1, NZD):
        returned(o).wait()
    e_ref[0] = back[...]
    for slab in range(2):
        for part in range(2):
            @pl.when(jnp.logical_not(stays(slab, part)))
            def _(slab=slab, part=part):
                sent(slab, part, sz).wait_send()

    for t in range(NZD):
        @pl.when(jnp.logical_not(jnp.logical_and(core == sz // 2, sz == t)))
        def _(t=t):
            sent(0, 0, t).wait_recv()

    for i in range(HALF):
        @pl.when(has_yr)
        def _(i=i):
            state(i).wait_send()

    x_ref[0] = xback[...]


def shards(g, c, f, d, ids, cnt, m):
    vm = pl.BlockSpec(memory_space=pltpu.VMEM)
    field = pltpu.VMEM((LAYERS, ROWS, NZ), jnp.float32)
    brick = pltpu.VMEM((DEEP, NY, NZ), jnp.float32)
    part = pltpu.VMEM((HALF, ROWS, NZ), jnp.float32)
    xf = pltpu.VMEM((2, ROWS, NZ), jnp.float32)
    zf = pltpu.VMEM((2, LAYERS, NZ), jnp.float32)
    z1 = pltpu.VMEM((LAYERS, NZ), jnp.float32)
    dma = pltpu.SemaphoreType.DMA
    out = jax.ShapeDtypeStruct(g.shape, jnp.float32)
    return pl.pallas_call(
        fine_kernel,
        out_shape=(out, out),
        in_specs=[vm] * 7,
        out_specs=(vm, vm),
        scratch_shapes=[field] * 9
        + [brick] * 2
        + [xf, xf, zf, zf, zf, zf, z1, z1]
        + [
            pltpu.VMEM((INCREMENTS, NZD, PAIRS, TILE, 128), jnp.float32),
            pltpu.VMEM((NZD, INCREMENTS, 128), jnp.int32),
            pltpu.VMEM((128, 128), jnp.float32),
        ]
        + [part] * 17
        + [
            pltpu.SMEM((NZD, INCREMENTS, 128), jnp.int32),
            dma((4, NZD)), dma((4, NZD)), dma((NZD,)), dma((NZD,)),
            dma((4, 2)), dma((4, 2)), dma((2, 2, 3)), dma((2, 2, 3)),
            dma((NZD,)), dma((NZD,)), dma,
            dma((3,)), dma((3,)), dma, dma, dma((HALF,)), dma((HALF,)),
            dma((HALF,)), dma((HALF,)), dma((2, 2)), dma((NZD,)),
        ],
        compiler_params=pltpu.CompilerParams(
            collective_id=0, has_side_effects=True, vmem_limit_bytes=48 << 20
        ),
    )(g, c, f, d, ids, cnt, m)


def solution(mesh):
    split = Mesh(
        mesh.devices.reshape(8, 2, 2, NXD, NZD), ("tm_0", "tm_1", "tm_2", "sx", "sz")
    )
    return jax.shard_map(
        shards,
        mesh=split,
        in_specs=(
            P(TM, SPACE, None, None),
            P(SPACE, None, None),
            P(TM, SPACE, None, None),
            P(TM, SPACE, None, None),
            P(TM, SPACE),
            P(TM, SPACE),
            P(TM, SPACE, None, None),
        ),
        out_specs=(P(TM, SPACE, None, None), P(TM, SPACE, None, None)),
        check_vma=False,
    )
```

```python
import jax
import jax.numpy as jnp
from jax import lax
from jax.experimental import pallas as pl
from jax.experimental.pallas import tpu as pltpu
from jax.sharding import Mesh
from jax.sharding import PartitionSpec as P

INCREMENTS = 8
SWEEPS = 4
TM = ("tm_0", "tm_1", "tm_2")
SPACE = ("sx", "sz")
MESH = pl.DeviceIdType.MESH
COND = 1.0

NZD = 4
NXD = 4
NYD = 8
DEEP = 4
LAYERS = DEEP * NZD
HALF = LAYERS // 2
ROWS = 32
NY = ROWS * NZD
NZ = 256
TILE = 64
MAXT = 8
PAIRS = MAXT // 2
LAST = 2 * INCREMENTS - 2


def kernel(
    g_ref, c_ref, f_ref, d_ref, ids_ref, cnt_ref, m_ref,
    x_ref, e_ref,
    p, a, b, inv, cap, src, rhs, dec, gp, back, xback,
    xlo, xhi, zlo, zhi, zs_lo, zs_hi, corner,
    inv_lo, inv_hi, cz_lo, cz_hi, fz_lo, fz_hi,
    rc_xl, rc_xh, rc_zl, rc_zh, rf_xl, rf_xh, rf_zl, rf_zh,
    rr_xl, rr_xh, rr_zl, rr_zh, w_xl, w_xh, w_zl, w_zh,
    mv, ids_v, cnt_v, bt, idv, dx,
    do, go, eo, a0, a1, ga0, ga1, ac, ao, ay, b0, bc, bo, pin, pout, x0, x1,
    ids_s,
    in_send, in_recv, c_send, c_recv, id_send, id_recv, h_send, h_recv, r_send, r_recv,
    b_send, b_recv, o_send, o_recv, loc,
    cs_send, cs_recv, s_send, s_recv, a_send, a_recv, z_send, z_recv, y_send, y_recv,
    x_send, x_recv,
):
    sx = lax.axis_index("sx")
    sz = lax.axis_index("sz")
    y = lax.axis_index("tm_0")
    zh = lax.axis_index("tm_1")
    core = lax.axis_index("tm_2")
    dz = 1 - 2 * zh
    q = (NZD - 1) * zh + dz * sz
    ring = NZD * zh + sz

    def quarter(device):
        return (NZD - 1) * zh + dz * device

    has_xl, has_xr = sx > 0, sx < NXD - 1
    has_bl, has_br = sz > 0, sz < NZD - 1
    has_zl, has_zr = q > 0, q < NZD - 1
    has_yl, has_yr = y > 0, y < NYD - 1
    across = {"tm_1": 1 - zh, "sz": NZD - 1 - sz}
    beside = {"tm_2": 1 - core}
    xl_at, xr_at = jnp.maximum(sx - 1, 0), jnp.minimum(sx + 1, NXD - 1)
    zl_at, zr_at = jnp.clip(sz - dz, 0, NZD - 1), jnp.clip(sz + dz, 0, NZD - 1)
    sides = (
        (has_xl, {"sx": xl_at}),
        (has_xr, {"sx": xr_at}),
        (jnp.logical_and(has_xl, has_zl), {"sx": xl_at, "sz": zl_at}),
        (jnp.logical_and(has_xl, has_zr), {"sx": xl_at, "sz": zr_at}),
        (jnp.logical_and(has_xr, has_zl), {"sx": xr_at, "sz": zl_at}),
        (jnp.logical_and(has_xr, has_zr), {"sx": xr_at, "sz": zr_at}),
        (has_yl, {"tm_0": jnp.maximum(y - 1, 0)}),
        (has_yr, {"tm_0": jnp.minimum(y + 1, NYD - 1)}),
    )

    barrier = pltpu.get_barrier_semaphore()
    expected = jnp.int32(4 * NZD - 1)
    for other in range(1, 4 * NZD):
        place = lax.rem(4 * NZD + 2 * ring + core - other, 4 * NZD)
        pl.semaphore_signal(
            barrier,
            inc=1,
            device_id={
                "tm_2": lax.rem(place, 2),
                "tm_1": place // (2 * NZD),
                "sz": lax.rem(place // 2, NZD),
            },
            device_id_type=MESH,
        )
    for there, where in sides:
        expected = expected + there.astype(jnp.int32)

        @pl.when(there)
        def _(where=where):
            pl.semaphore_signal(barrier, inc=1, device_id=where, device_id_type=MESH)

    own_rows = pl.ds(ROWS * q, ROWS)
    mine = pl.ds(DEEP * sz, DEEP)
    local = [
        pltpu.make_async_copy(ids_ref, ids_v, loc.at[0]),
        pltpu.make_async_copy(cnt_ref, cnt_v, loc.at[1]),
        pltpu.make_async_copy(m_ref, mv, loc.at[2]),
        pltpu.make_async_copy(g_ref.at[0, :, own_rows, :], p.at[mine], loc.at[3]),
        pltpu.make_async_copy(f_ref.at[0, :, own_rows, :], src.at[mine], loc.at[4]),
        pltpu.make_async_copy(c_ref.at[:, own_rows, :], cap.at[mine], loc.at[5]),
        pltpu.make_async_copy(d_ref.at[0, :, own_rows, :], dec.at[mine], loc.at[6]),
    ]
    for copy in local:
        copy.start()
    local[0].wait()
    local[1].wait()
    idv[sz] = jnp.zeros((2 * INCREMENTS, 128), jnp.int32)
    idv[sz, 0:INCREMENTS, 0:MAXT] = ids_v[...]
    idv[sz, INCREMENTS : INCREMENTS + 1, 0:INCREMENTS] = cnt_v[...]
    pl.semaphore_wait(barrier, expected)

    def dealt(n, o):
        to = lax.rem(sz + o, NZD)
        source = (g_ref.at[0], f_ref.at[0], d_ref.at[0])[n]
        target = (p, src, dec)[n]
        return pltpu.make_async_remote_copy(
            src_ref=source.at[:, pl.ds(ROWS * quarter(to), ROWS), :],
            dst_ref=target.at[mine],
            send_sem=in_send.at[n, o],
            recv_sem=in_recv.at[n, o],
            device_id={"sz": to},
            device_id_type=MESH,
        )

    steps = (1, -1, 2 - 4 * core)

    def capacity_in(n):
        to = lax.rem(ring + steps[n] + 2 * NZD, 2 * NZD)
        to_zh, to_sz = to // NZD, lax.rem(to, NZD)
        to_q = (NZD - 1) * to_zh + (1 - 2 * to_zh) * to_sz
        return pltpu.make_async_remote_copy(
            src_ref=c_ref.at[pl.ds(2 * core, 2), pl.ds(ROWS * to_q, ROWS), :],
            dst_ref=cap.at[pl.ds(DEEP * sz + 2 * core, 2)],
            send_sem=c_send.at[0, n],
            recv_sem=c_recv.at[0, n],
            device_id={"tm_1": to_zh, "sz": to_sz},
            device_id_type=MESH,
        )

    def capacity_on(n):
        origin = lax.rem(ring - steps[n] + 2 * NZD, NZD)
        part = cap.at[pl.ds(DEEP * origin + 2 * core, 2)]
        return pltpu.make_async_remote_copy(
            src_ref=part,
            dst_ref=part,
            send_sem=c_send.at[1, n],
            recv_sem=c_recv.at[1, n],
            device_id=beside,
            device_id_type=MESH,
        )

    def listed(o):
        to = lax.rem(sz + o, NZD)
        return pltpu.make_async_remote_copy(
            src_ref=idv.at[sz],
            dst_ref=idv.at[sz],
            send_sem=id_send.at[o],
            recv_sem=id_recv.at[o],
            device_id={"sz": to},
            device_id_type=MESH,
        )

    for n in range(3):
        capacity_in(n).start()
    for n in range(2):
        for o in range(1, NZD):
            dealt(n, o).start()
    for o in range(1, NZD):
        listed(o).start()

    def block_copy(n, d, r):
        brick = jnp.clip(sz - r if d == 0 else sz + r, 0, NZD - 1)
        part = bt.at[n // 2, brick, pl.ds(2 * lax.rem(n, 2), 2)]
        return pltpu.make_async_remote_copy(
            src_ref=part,
            dst_ref=part,
            send_sem=b_send.at[lax.rem(n, 4), d, r],
            recv_sem=b_recv.at[lax.rem(n, 4), d, r],
            device_id={"sz": jnp.clip(sz + 1 if d == 0 else sz - 1, 0, NZD - 1)},
            device_id_type=MESH,
        )

    def block_start(n, r):
        @pl.when(jnp.logical_and(sz - r >= 0, has_br))
        def _():
            block_copy(n, 0, r).start()

        @pl.when(jnp.logical_and(sz + r < NZD, has_bl))
        def _():
            block_copy(n, 1, r).start()

    def block_wait(n, r):
        @pl.when(jnp.logical_and(sz - r >= 0, has_br))
        def _():
            block_copy(n, 0, r).wait_send()

        @pl.when(jnp.logical_and(sz + r < NZD, has_bl))
        def _():
            block_copy(n, 1, r).wait_send()

        @pl.when(sz - 1 - r >= 0)
        def _():
            block_copy(n, 0, r).wait_recv()

        @pl.when(sz + 1 + r < NZD)
        def _():
            block_copy(n, 1, r).wait_recv()

    local[2].wait()

    def turned(k, carry):
        for i in range(PAIRS):
            two = mv[k, 2 * i : 2 * i + 2].reshape(2 * TILE, TILE)
            bt[k, sz, i] = two.T
        return carry

    lax.fori_loop(0, INCREMENTS, turned, 0)
    block_start(0, 0)
    block_start(1, 0)
    for ref, have in ((xlo, has_xl), (xhi, has_xr), (zlo, has_zl), (zhi, has_zr)):
        @pl.when(jnp.logical_not(have))
        def _(ref=ref):
            ref[...] = jnp.zeros(ref.shape, jnp.float32)

    for refs, have in (
        ((rc_xl, rf_xl), has_xl),
        ((rc_xh, rf_xh), has_xr),
        ((rc_zl, rf_zl), has_zl),
        ((rc_zh, rf_zh), has_zr),
    ):
        @pl.when(jnp.logical_not(have))
        def _(refs=refs):
            for ref in refs:
                ref[...] = jnp.zeros(ref.shape, jnp.float32)

    for n in range(4):
        @pl.when(jnp.logical_not(sides[2 + n][0]))
        def _(n=n):
            for slot in range(2):
                corner[slot, n] = jnp.zeros((8, NZ), jnp.float32)

    dx[...] = jnp.zeros((128, 128), jnp.float32)
    for copy in local[3:]:
        copy.wait()
    for n in range(3):
        capacity_in(n).wait()
    for n in range(3):
        capacity_on(n).start()
    for n in range(3):
        capacity_on(n).wait()

    def inverses(l, carry):
        inv[l] = 1.0 / (cap[l] + 6.0 * COND)
        return carry

    lax.fori_loop(0, LAYERS, inverses, 0)
    inv_lo[...] = inv[:, 0, :]
    inv_hi[...] = inv[:, ROWS - 1, :]
    cz_lo[...] = cap[:, 0, :]
    cz_hi[...] = cap[:, ROWS - 1, :]
    for n in range(2):
        for o in range(1, NZD):
            dealt(n, o).wait()
    for o in range(1, NZD):
        listed(o).wait()
    lists = pltpu.make_async_copy(idv, ids_s, loc.at[0])
    lists.start()
    fz_lo[...] = src[:, 0, :]
    fz_hi[...] = src[:, ROWS - 1, :]

    def faces(slot):
        zs_lo[slot, 0] = p[:, 0, :]
        zs_lo[slot, 1] = p[:, 1, :]
        zs_hi[slot, 0] = p[:, ROWS - 1, :]
        zs_hi[slot, 1] = p[:, ROWS - 2, :]

    faces(0)

    def moved(source, target, sems, where):
        return pltpu.make_async_remote_copy(
            src_ref=source,
            dst_ref=target,
            send_sem=sems[0],
            recv_sem=sems[1],
            device_id=where,
            device_id_type=MESH,
        )

    to_xl, to_xr = {"sx": xl_at}, {"sx": xr_at}
    to_zl, to_zr = {"sz": zl_at}, {"sz": zr_at}

    def rims():
        out = []
        for n, (field, lo, hi, xl, xh, zl, zh_) in enumerate((
            (cap, cz_lo, cz_hi, rc_xl, rc_xh, rc_zl, rc_zh),
            (src, fz_lo, fz_hi, rf_xl, rf_xh, rf_zl, rf_zh),
        )):
            for m, (sends, gets, source, target, where) in enumerate((
                (has_xl, has_xr, field.at[0], xh, to_xl),
                (has_xr, has_xl, field.at[LAYERS - 1], xl, to_xr),
                (has_zl, has_zr, lo, zh_, to_zl),
                (has_zr, has_zl, hi, zl, to_zr),
            )):
                sems = (r_send.at[n, m], r_recv.at[n, m])
                out.append((sends, gets, moved(source, target, sems, where)))
        return out

    def begin(copies):
        for sends, unused, copy in copies:
            @pl.when(sends)
            def _(copy=copy):
                copy.start()

    def end(copies):
        for sends, gets, copy in copies:
            @pl.when(gets)
            def _(copy=copy):
                copy.wait_recv()

            @pl.when(sends)
            def _(copy=copy):
                copy.wait_send()

    def halo(field, slot):
        def sems(n):
            return h_send.at[n, slot], h_recv.at[n, slot]

        ll, lh, hl, hh = sides[2][0], sides[3][0], sides[4][0], sides[5][0]
        at = [side[1] for side in sides[2:6]]
        top, low = pl.ds(0, 8), pl.ds(ROWS - 8, 8)
        last = LAYERS - 1
        return [
            (has_xl, has_xr, moved(field.at[pl.ds(0, 2)], xhi.at[slot], sems(0), to_xl)),
            (has_xr, has_xl, moved(field.at[pl.ds(last - 1, 2)], xlo.at[slot], sems(1), to_xr)),
            (has_zl, has_zr, moved(zs_lo.at[slot], zhi.at[slot], sems(2), to_zl)),
            (has_zr, has_zl, moved(zs_hi.at[slot], zlo.at[slot], sems(3), to_zr)),
            (ll, hh, moved(field.at[0, top], corner.at[slot, 3], sems(4), at[0])),
            (lh, hl, moved(field.at[0, low], corner.at[slot, 2], sems(5), at[1])),
            (hl, lh, moved(field.at[last, top], corner.at[slot, 1], sems(6), at[2])),
            (hh, ll, moved(field.at[last, low], corner.at[slot, 0], sems(7), at[3])),
        ]

    row = lax.broadcasted_iota(jnp.int32, (ROWS, NZ), 0)
    lane = lax.broadcasted_iota(jnp.int32, (ROWS, NZ), 1)
    layer_of = lax.broadcasted_iota(jnp.int32, (LAYERS, NZ), 0)
    lane_z = lax.broadcasted_iota(jnp.int32, (LAYERS, NZ), 1)

    def along(w, index):
        left = jnp.where(index == 0, 0.0, pltpu.roll(w, 1, 1))
        return left + jnp.where(index == NZ - 1, 0.0, pltpu.roll(w, NZ - 1, 1))

    def between(w, index, before, after):
        n = w.shape[0]
        up = jnp.where(index == 0, before, pltpu.roll(w, 1, 0))
        return up + jnp.where(index == n - 1, after, pltpu.roll(w, n - 1, 0))

    def inner(old, new, first):
        for l in range(LAYERS):
            w = old[l]
            t = between(w, row, 0.0, 0.0) + along(w, lane)
            if l > 0:
                t = t + old[l - 1]
            if l < LAYERS - 1:
                t = t + old[l + 1]
            if first:
                r = cap[l] * w + src[l]
                rhs[l] = r
            else:
                r = rhs[l]
            new[l] = (r + COND * t) * inv[l]

    def outer(new, xl, xh, zl, zh_):
        new[0] = new[0] + COND * (inv[0] * xl)
        new[LAYERS - 1] = new[LAYERS - 1] + COND * (inv[LAYERS - 1] * xh)
        lo = new[:, 0, :] + COND * (inv_lo[...] * zl)
        hi = new[:, ROWS - 1, :] + COND * (inv_hi[...] * zh_)
        new[:, 0, :] = lo
        new[:, ROWS - 1, :] = hi
        return lo, hi

    def inverse(c, have):
        return jnp.where(have, 1.0 / (c + 6.0 * COND), 0.0)

    def two_sweeps(old, mid, new, slot, first, early, late):
        copies = halo(old, slot)
        begin(copies)
        early()
        inner(old, mid, first)
        end(copies)
        late()
        xl, xh, zl, zh_ = xlo[slot, 1], xhi[slot, 0], zlo[slot, 0], zhi[slot, 0]
        outer(mid, xl, xh, zl, zh_)
        if first:
            rr_xl[...] = rc_xl[...] * xl + rf_xl[...]
            rr_xh[...] = rc_xh[...] * xh + rf_xh[...]
            rr_zl[...] = rc_zl[...] * zl + rf_zl[...]
            rr_zh[...] = rc_zh[...] * zh_ + rf_zh[...]
        ll, lh = corner[slot, 0, 7:8, :], corner[slot, 1, 0:1, :]
        hl, hh = corner[slot, 2, 7:8, :], corner[slot, 3, 0:1, :]
        t = xlo[slot, 0] + old[0] + between(xl, row, ll, lh) + along(xl, lane)
        w_xl[...] = (rr_xl[...] + COND * t) * inverse(rc_xl[...], has_xl)
        t = xhi[slot, 1] + old[LAYERS - 1] + between(xh, row, hl, hh) + along(xh, lane)
        w_xh[...] = (rr_xh[...] + COND * t) * inverse(rc_xh[...], has_xr)
        t = zlo[slot, 1] + zs_lo[slot, 0] + between(zl, layer_of, ll, hl) + along(zl, lane_z)
        w_zl[...] = (rr_zl[...] + COND * t) * inverse(rc_zl[...], has_zl)
        t = zhi[slot, 1] + zs_hi[slot, 0] + between(zh_, layer_of, lh, hh) + along(zh_, lane_z)
        w_zh[...] = (rr_zh[...] + COND * t) * inverse(rc_zh[...], has_zr)
        inner(mid, new, False)
        lo, hi = outer(new, w_xl[...], w_xh[...], w_zl[...], w_zh[...])
        if first:
            zs_lo[1 - slot, 0] = lo
            zs_hi[1 - slot, 0] = hi
            zs_lo[1 - slot, 1] = new[:, 1, :]
            zs_hi[1 - slot, 1] = new[:, ROWS - 2, :]

    lane_r = lax.broadcasted_iota(jnp.int32, (1, 128), 1) < TILE
    lane_c = lax.broadcasted_iota(jnp.int32, (TILE, 128), 1) < TILE
    cell = lax.broadcasted_iota(jnp.int32, (DEEP * ROWS, NZ), 0)

    def fix(k):
        places = []
        for brick in range(NZD):
            count = ids_s[brick, INCREMENTS, k]
            for i in range(PAIRS):
                halves = []
                for odd in range(2):
                    slot = 2 * i + odd
                    tile = ids_s[brick, k, slot]
                    quad = lax.rem(tile, 4)
                    line = lax.rem(tile // 4, NY) - ROWS * q
                    layer = tile // (4 * NY)
                    owned = (line >= 0) & (line < ROWS) & (slot < count)
                    line_in = jnp.clip(line, 0, ROWS - 1)
                    where = DEEP * brick + layer
                    d = b[where, pl.ds(line_in, 1), :] - p[where, pl.ds(line_in, 1), :]
                    h = jnp.where(quad >= 2, d[:, 128:], d[:, :128])
                    turn = lax.rem(quad, 2) != odd
                    h = jnp.where(turn, pltpu.roll(h, TILE, 1), h)
                    halves.append(h)
                    places.append((jnp.where(owned, layer * ROWS + line_in, -1), quad, turn))
                dx[brick * PAIRS + i : brick * PAIRS + i + 1, :] = jnp.where(
                    lane_r, halves[0], halves[1]
                )
        columns = dx[...].T
        for brick in range(NZD):
            total = b[DEEP * brick : DEEP * (brick + 1)].reshape(DEEP * ROWS, NZ)
            for i in range(PAIRS):
                at = brick * PAIRS + i
                d = jnp.where(
                    lane_c,
                    jnp.broadcast_to(columns[0:TILE, at : at + 1], (TILE, 128)),
                    jnp.broadcast_to(columns[TILE : 2 * TILE, at : at + 1], (TILE, 128)),
                )
                sums = jnp.sum(bt[k, brick, i] * d, axis=0, keepdims=True)
                for odd in range(2):
                    place, quad, turn = places[brick * MAXT + 2 * i + odd]
                    h = jnp.where(turn, pltpu.roll(sums, TILE, 1), sums)
                    right = lax.rem(quad, 2) == 1
                    h = jnp.where(lane_r != right, h, 0.0)
                    wide = jnp.concatenate(
                        [jnp.where(quad < 2, h, 0.0), jnp.where(quad < 2, 0.0, h)], axis=1
                    )
                    total = total + jnp.where(cell == place, wide, 0.0)
            p[DEEP * brick : DEEP * (brick + 1)] = total.reshape(DEEP, ROWS, NZ)
        faces(0)

    half = pl.ds(HALF * core, HALF)
    rest = pl.ds(HALF * (1 - core), HALF)
    first_slab = jnp.logical_and(y == 0, zh == 0)

    def swapped(n, source, target):
        return pltpu.make_async_remote_copy(
            src_ref=source.at[rest],
            dst_ref=target,
            send_sem=cs_send.at[n],
            recv_sem=cs_recv.at[n],
            device_id=beside,
            device_id_type=MESH,
        )

    def factors(n):
        return swapped(n, (dec, gp)[n], (do, go)[n])

    def factors_ready():
        for i in range(HALF):
            own_d, own_g = dec[HALF * core + i], gp[HALF * core + i]
            d0 = jnp.where(core == 0, own_d, do[i])
            d1 = jnp.where(core == 0, do[i], own_d)
            g0 = jnp.where(core == 0, own_g, go[i])
            g1 = jnp.where(core == 0, go[i], own_g)
            d0 = jnp.where(first_slab, 0.0, d0)
            a0[i] = d0
            a1[i] = d1
            ga0[i] = d0 * g0
            ga1[i] = d1 * g1
            ac[i] = d0 * d1
            pout[i] = g0

    def scales():
        return pltpu.make_async_remote_copy(
            src_ref=ac,
            dst_ref=ao,
            send_sem=a_send,
            recv_sem=a_recv,
            device_id=across,
            device_id_type=MESH,
        )

    def shift(i):
        return pltpu.make_async_remote_copy(
            src_ref=bc.at[i],
            dst_ref=bo.at[i],
            send_sem=z_send.at[i],
            recv_sem=z_recv.at[i],
            device_id=across,
            device_id_type=MESH,
        )

    def state(i):
        return pltpu.make_async_remote_copy(
            src_ref=pout.at[i],
            dst_ref=pin.at[i],
            send_sem=y_send.at[i],
            recv_sem=y_recv.at[i],
            device_id={"tm_0": jnp.minimum(y + 1, NYD - 1)},
            device_id_type=MESH,
        )

    def swapped_end(i):
        return pltpu.make_async_remote_copy(
            src_ref=p.at[HALF * (1 - core) + i],
            dst_ref=eo.at[i],
            send_sem=s_send.at[i],
            recv_sem=s_recv.at[i],
            device_id=beside,
            device_id_type=MESH,
        )

    begin(rims())
    lists.wait()

    def traffic(n):
        @pl.when(n == 0)
        def _():
            block_wait(0, 0)
            block_start(0, 1)

        @pl.when(n < LAST + 1)
        def _():
            block_wait(n + 1, 0)
            block_start(n + 1, 1)

        @pl.when(n == 1)
        def _():
            block_start(0, 2)

        @pl.when(n > 0)
        def _():
            block_start(n, 2)

        @pl.when(n < LAST)
        def _():
            block_start(n + 2, 0)

    def step(k, carry):
        def early_one():
            @pl.when(k > 0)
            def _():
                block_wait(2 * k, 1)

            traffic(2 * k)

            @pl.when(k == 0)
            def _():
                gp[...] = p[...]

        def early_two():
            @pl.when(k == 0)
            def _():
                block_wait(0, 1)
                block_wait(1, 1)

            @pl.when(k > 0)
            def _():
                block_wait(2 * k + 1, 1)

            traffic(2 * k + 1)

            for o in range(1, NZD):
                @pl.when(k == o)
                def _(o=o):
                    dealt(2, o).start()

            @pl.when(k == 5)
            def _():
                for o in range(1, NZD):
                    dealt(2, o).wait()
                factors(0).start()
                factors(1).start()

            @pl.when(k == 6)
            def _():
                factors(0).wait()
                factors(1).wait()
                factors_ready()
                scales().start()

            @pl.when(k == 7)
            def _():
                scales().wait()
                for i in range(HALF):
                    ay[i] = ac[i] * ao[i]

        def late_one():
            @pl.when(k == 0)
            def _():
                end(rims())

        two_sweeps(p, a, b, 0, True, early_one, late_one)
        two_sweeps(b, a, b, 1, False, early_two, lambda: None)
        block_wait(2 * k, 2)
        block_wait(2 * k + 1, 2)
        fix(k)
        return carry

    lax.fori_loop(0, INCREMENTS, step, 0)

    def returned(o):
        to = lax.rem(sz + o, NZD)
        return pltpu.make_async_remote_copy(
            src_ref=p.at[pl.ds(DEEP * to, DEEP)],
            dst_ref=back.at[:, own_rows, :],
            send_sem=o_send.at[o],
            recv_sem=o_recv.at[o],
            device_id={"sz": to},
            device_id_type=MESH,
        )

    for i in range(HALF):
        swapped_end(i).start()
    for i in range(HALF):
        swapped_end(i).wait()
        own = p[HALF * core + i]
        s0 = jnp.where(core == 0, own, eo[i]) - ga0[i]
        s1 = jnp.where(core == 0, eo[i], own) - ga1[i]
        b0[i] = s0
        bc[i] = a1[i] * s0 + s1
        shift(i).start()
    for o in range(1, NZD):
        returned(o).start()
    back[:, own_rows, :] = p[mine]

    def sent(slab, i, source):
        return pltpu.make_async_remote_copy(
            src_ref=(x0, x1)[slab].at[i],
            dst_ref=xback.at[i % DEEP, pl.ds(ROWS * quarter(source), ROWS), :],
            send_sem=x_send.at[slab, i],
            recv_sem=x_recv.at[source, i % DEEP],
            device_id={"tm_2": slab, "sz": 2 * core + i // DEEP},
            device_id_type=MESH,
        )

    def stays(slab, i):
        return jnp.logical_and(core == slab, sz == 2 * core + i // DEEP)

    for i in range(HALF):
        shift(i).wait()

        @pl.when(has_yl)
        def _(i=i):
            state(i).wait_recv()
            pout[i] = pin[i]

        before = pout[i]
        shift_0 = jnp.where(zh == 0, bc[i], bo[i])
        shift_1 = jnp.where(zh == 0, bo[i], bc[i])
        scale_0 = jnp.where(zh == 0, ac[i], ao[i])
        scale_1 = jnp.where(zh == 0, ao[i], ac[i])
        pout[i] = ay[i] * before + (scale_1 * shift_0 + shift_1)

        @pl.when(has_yr)
        def _(i=i):
            state(i).start()

        start = jnp.where(zh == 0, before, scale_0 * before + shift_0)
        x0[i] = start
        x1[i] = a0[i] * start + b0[i]
        for slab in range(2):
            @pl.when(jnp.logical_not(stays(slab, i)))
            def _(slab=slab, i=i):
                sent(slab, i, sz).start()

            @pl.when(stays(slab, i))
            def _(slab=slab, i=i):
                xback[i % DEEP, own_rows, :] = (x0, x1)[slab][i]

    for o in range(1, NZD):
        returned(o).wait()
    e_ref[0] = back[...]
    for slab in range(2):
        for i in range(HALF):
            @pl.when(jnp.logical_not(stays(slab, i)))
            def _(slab=slab, i=i):
                sent(slab, i, sz).wait_send()

    for t in range(NZD):
        @pl.when(jnp.logical_not(jnp.logical_and(core == sz // 2, sz == t)))
        def _(t=t):
            for i in range(DEEP):
                sent(0, i, t).wait_recv()

    for i in range(HALF):
        @pl.when(has_yr)
        def _(i=i):
            state(i).wait_send()

    x_ref[0] = xback[...]


def shards(g, c, f, d, ids, cnt, m):
    hbm = pl.BlockSpec(memory_space=pltpu.HBM)
    vm = pl.BlockSpec(memory_space=pltpu.VMEM)

    def f32(*shape):
        return pltpu.VMEM(shape, jnp.float32)

    field = f32(LAYERS, ROWS, NZ)
    brick = f32(DEEP, NY, NZ)
    part = f32(HALF, ROWS, NZ)
    xf = f32(2, 2, ROWS, NZ)
    zf = f32(2, 2, LAYERS, NZ)
    x1, z1 = f32(ROWS, NZ), f32(LAYERS, NZ)
    dma = pltpu.SemaphoreType.DMA
    out = jax.ShapeDtypeStruct(g.shape, jnp.float32)
    return pl.pallas_call(
        kernel,
        out_shape=(out, out),
        in_specs=[hbm] * 7,
        out_specs=(vm, vm),
        scratch_shapes=[field] * 9
        + [brick] * 2
        + [xf, xf, zf, zf, zf, zf, f32(2, 4, 8, NZ)]
        + [z1] * 6
        + [x1, x1, z1, z1] * 4
        + [
            f32(INCREMENTS, MAXT, TILE, TILE),
            pltpu.VMEM((INCREMENTS, MAXT), jnp.int32),
            pltpu.VMEM((1, INCREMENTS), jnp.int32),
            f32(INCREMENTS, NZD, PAIRS, TILE, 128),
            pltpu.VMEM((NZD, 2 * INCREMENTS, 128), jnp.int32),
            f32(128, 128),
        ]
        + [part] * 17
        + [
            pltpu.SMEM((NZD, 2 * INCREMENTS, 128), jnp.int32),
            dma((3, NZD)), dma((3, NZD)), dma((2, 3)), dma((2, 3)), dma((NZD,)), dma((NZD,)),
            dma((8, 2)), dma((8, 2)), dma((2, 4)), dma((2, 4)),
            dma((4, 2, 3)), dma((4, 2, 3)),
            dma((NZD,)), dma((NZD,)), dma((7,)),
            dma((2,)), dma((2,)), dma((HALF,)), dma((HALF,)), dma, dma, dma((HALF,)), dma((HALF,)),
            dma((HALF,)), dma((HALF,)), dma((2, HALF)), dma((NZD, DEEP)),
        ],
        compiler_params=pltpu.CompilerParams(
            collective_id=0, has_side_effects=True, vmem_limit_bytes=48 << 20
        ),
    )(g, c, f, d, ids, cnt.reshape(1, INCREMENTS), m)


def solution(mesh):
    split = Mesh(
        mesh.devices.reshape(8, 2, 2, NXD, NZD), ("tm_0", "tm_1", "tm_2", "sx", "sz")
    )
    return jax.shard_map(
        shards,
        mesh=split,
        in_specs=(
            P(TM, SPACE, None, None),
            P(SPACE, None, None),
            P(TM, SPACE, None, None),
            P(TM, SPACE, None, None),
            P(TM, SPACE),
            P(TM, SPACE),
            P(TM, SPACE, None, None),
        ),
        out_specs=(P(TM, SPACE, None, None), P(TM, SPACE, None, None)),
        check_vma=False,
    )
```
